32 devices in a mesh: wide: 8 (over z, x), narrow: 4 (over y, core).
Axes of the slice: x: 2, y: 2, z: 4, core: 2. Of those that a mesh axis runs over, the one named last changes fastest.
Arguments:
- fields: bfloat16 [256, 32768], P('wide', 'narrow'), may hold values from -8 to 8
- counts: int32 [4, 8], P(None, 'wide'), may hold values from 1 to 8, as said below
- obs_index: int32 [4, 8, 8, 512], P('narrow', 'wide'), may hold values from 0 to 1023
- obs_value: float32 [4, 8, 8, 512], P('narrow', 'wide'), may hold values from -6 to 6
- obs_weight: bfloat16 [4, 8, 8, 512], P('narrow', 'wide'), may hold values from 1 to 16
Outputs:
- analysis: bfloat16 [256, 32768], P('wide', 'narrow')
The draws below stay inside these ranges and needn't reach their ends.
Inputs may be any that keep to these rules, and one draw needn't show every extreme that they name: `counts`: tiles with the same wide index form a group of 4; in each group exactly one tile owns 6 to 8 patches and every other tile owns 1 to 4. `obs_index`: slots numbered at or beyond the tile's count are never read.
All inputs are finite; a program needn't handle non-finite values.
Results may differ from the reference program's by a relative error of at most 0.009.
Values may be sent and summed in bfloat16 or wider, within the bound.
No kernel may reach another device: no remote copies, remote signals or barrier semaphores. Data moves between devices by JAX's collectives and lax.ppermute only.
A program may use at most 64 MiB of HBM per device.

```python
import math
import jax
import jax.numpy as jnp
from jax import lax

K = 256
NOBS = 512
PMAX = 8
LOCAL = 5
NS_ITERS = 6
CELL_DEV = 1024
NCELL = 32768
N_WIDE = 8
N_NARROW = 4


def draw_fields(key, part):
    key_base, key_scale, key_noise = jax.random.split(jax.random.fold_in(key, 11), 3)
    base_field = jax.random.normal(key_base, (1, NCELL), jnp.float32)
    spread = jnp.exp(jax.random.uniform(key_scale, (1, NCELL), jnp.float32, math.log(0.3), math.log(1.5)))
    noise = jax.random.normal(key_noise, (K, NCELL), jnp.float32)
    return jnp.clip(base_field + spread * noise, -8.0, 8.0).astype(jnp.bfloat16)


def draw_counts(key, part):
    key_heavy, key_pick, key_light = jax.random.split(jax.random.fold_in(key, 23), 3)
    heavy_row = jax.random.randint(key_pick, (1, N_WIDE), 0, N_NARROW)
    heavy_count = jax.random.randint(key_heavy, (1, N_WIDE), LOCAL + 1, PMAX + 1)
    light_count = jax.random.randint(key_light, (N_NARROW, N_WIDE), 1, LOCAL)
    row_ids = lax.broadcasted_iota(jnp.int32, (N_NARROW, N_WIDE), 0)
    return jnp.where(row_ids == heavy_row, heavy_count, light_count).astype(jnp.int32)


def set_ends(values, stream_key, low, high):
    longest = values.shape.index(max(values.shape))
    spots = []
    for shift in (0, 1):
        where = [jax.random.randint(jax.random.fold_in(stream_key, axis), (), 0, length) for axis, length in enumerate(values.shape)]
        where[longest] = (where[longest] + shift) % values.shape[longest]
        spots.append(tuple(where))
    return values.at[spots[0]].set(low).at[spots[1]].set(high)


def levels(own_key, shape, shards, low, top_value):
    level, own = 1.0, jax.random.fold_in(own_key, 6)
    for axis_at, shards_of in shards:
        steps = jnp.exp(jax.random.uniform(jax.random.fold_in(own, axis_at), (shards_of,), jnp.float32, low / len(shards), top_value / len(shards)))
        level = level * jnp.repeat(steps, shape[axis_at] // shards_of).reshape([-1 if axis == axis_at else 1 for axis in range(len(shape))])
    return level


def gaussian(own_key, dims, width, reach, cuts=(), kind=jnp.bfloat16):
    array = jax.random.normal(own_key, dims, jnp.float32) * width
    if len(cuts) > 0:
        array = levels(own_key, dims, cuts, -0.22, 0.18) * array
    return jnp.clip(array, min=-reach, max=reach).astype(kind)


def setup_inputs(seed: int = 0) -> dict:
    key_list = jax.random.split(jax.random.key(seed), 6)
    fields = draw_fields(jax.random.fold_in(key_list[5], 71), 0)
    counts = draw_counts(jax.random.fold_in(key_list[5], 71), 0)
    obs_index = set_ends(jax.random.randint(key_list[2], (N_NARROW, N_WIDE, PMAX, NOBS), 0, CELL_DEV), jax.random.fold_in(key_list[2], 1), 0, CELL_DEV - 1).astype(jnp.int32)
    obs_value = gaussian(key_list[3], (N_NARROW, N_WIDE, PMAX, NOBS), 1.5, 6.0, ((0, 4), (1, 8)), jnp.float32)
    obs_weight = jnp.clip(jnp.exp(math.log(16.0) - 2.7725887 * jax.random.uniform(key_list[4], (N_NARROW, N_WIDE, PMAX, NOBS), jnp.float32) ** levels(key_list[4], (N_NARROW, N_WIDE, PMAX, NOBS), ((0, 4), (1, 8)), -0.2, 0.2)), 1.0, 16.0).astype(jnp.bfloat16)
    return dict(fields=fields, counts=counts, obs_index=obs_index, obs_value=obs_value, obs_weight=obs_weight)


def prepare_slots(observed, weighted, innovation):
    members = observed.shape[0]
    highest = lax.Precision.HIGHEST
    obs_float = observed.astype(jnp.float32)
    identity_matrix = jnp.eye(members, dtype=jnp.float32)
    gram_matrix = jnp.einsum('ksn,lsn->skl', weighted.astype(jnp.float32), obs_float, precision=highest)
    gram_matrix = gram_matrix + (members - 1.0) * identity_matrix
    scale_value = jnp.sqrt(lax.optimization_barrier(jnp.sum(gram_matrix * gram_matrix, axis=(1, 2))))
    right_side = jnp.einsum('ksn,sn->sk', obs_float, innovation.astype(jnp.float32), precision=highest)
    iterate = (gram_matrix / scale_value[:, None, None]).astype(jnp.bfloat16)
    return (iterate, scale_value, right_side)

def newton_steps(iterate):
    members = iterate.shape[1]
    highest = lax.Precision.HIGHEST
    identity_matrix = jnp.eye(members, dtype=jnp.float32)
    root_matrix = jnp.broadcast_to(identity_matrix, iterate.shape).astype(jnp.bfloat16)
    for iteration in range(NS_ITERS):
        product = jnp.einsum('skl,slm->skm', root_matrix.astype(jnp.float32), iterate.astype(jnp.float32), precision=highest)
        factor = (1.5 * identity_matrix - 0.5 * product).astype(jnp.bfloat16)
        factor_float = factor.astype(jnp.float32)
        next_iterate = jnp.einsum('skl,slm->skm', iterate.astype(jnp.float32), factor_float, precision=highest).astype(jnp.bfloat16)
        root_matrix = jnp.einsum('skl,slm->skm', factor_float, root_matrix.astype(jnp.float32), precision=highest).astype(jnp.bfloat16)
        iterate = next_iterate
    return root_matrix

def finish_slots(root_matrix, scale_value, right_side):
    members = root_matrix.shape[1]
    highest = lax.Precision.HIGHEST
    root_float = root_matrix.astype(jnp.float32)
    inner_vector = jnp.einsum('skl,sl->sk', root_float, right_side, precision=highest)
    mean_shift = jnp.einsum('skl,sl->sk', root_float, inner_vector, precision=highest) / scale_value[:, None]
    patch_weight = jnp.sqrt((members - 1.0) / scale_value)[:, None, None] * root_float + mean_shift[:, :, None]
    return patch_weight.astype(jnp.bfloat16)

def solve_slots(observed, weighted, innovation):
    iterate, scale_value, right_side = prepare_slots(observed, weighted, innovation)
    return finish_slots(newton_steps(iterate), scale_value, right_side)

def combine_blocks(anomaly, member_mean, patch_weights, patch_count):
    members, cell_total = anomaly.shape
    slot_total = patch_weights.shape[0]
    block_ids = jnp.arange(slot_total, dtype=jnp.int32)
    owner_patch = block_ids * patch_count // slot_total
    pick_table = (owner_patch[:, None] == block_ids[None, :]).astype(jnp.float32)
    chosen = jnp.einsum('bp,pkl->bkl', pick_table, patch_weights.astype(jnp.float32), precision=lax.Precision.HIGHEST)
    blocks = anomaly.astype(jnp.float32).reshape(members, slot_total, cell_total // slot_total)
    result = jnp.einsum('bkl,kbc->lbc', chosen, blocks, precision=lax.Precision.HIGHEST)
    result = result + member_mean.reshape(1, slot_total, cell_total // slot_total)
    return result.reshape(members, cell_total).astype(jnp.bfloat16)

def analyse_tile(tile_fields, patch_count, indices, obs_values, weight_tile):
    members = tile_fields.shape[0]
    member_mean = lax.optimization_barrier(jnp.sum(tile_fields.astype(jnp.float32), axis=0)) / members
    anomaly = (tile_fields.astype(jnp.float32) - member_mean[None, :]).astype(jnp.bfloat16)
    observed = jnp.take(anomaly, indices, axis=1)
    obs_mean = jnp.take(member_mean, indices, axis=0)
    weight_float = weight_tile.astype(jnp.float32)
    weighted = (observed.astype(jnp.float32) * weight_float[None]).astype(jnp.bfloat16)
    innovation = (weight_float * (obs_values - obs_mean)).astype(jnp.bfloat16)
    patch_weights = solve_slots(observed, weighted, innovation)
    return combine_blocks(anomaly, member_mean, patch_weights, patch_count)

def reference(fields, counts, obs_index, obs_value, obs_weight):
    tile_total = N_NARROW * N_WIDE
    counts_flat = counts.reshape(tile_total)
    index_flat = obs_index.reshape(tile_total, PMAX, NOBS)
    value_flat = obs_value.reshape(tile_total, PMAX, NOBS)
    weight_flat = obs_weight.reshape(tile_total, PMAX, NOBS)

    def one_tile(tile_number, output):
        tile_number = tile_number.astype(jnp.int32)
        start = (tile_number * CELL_DEV).astype(jnp.int32)
        tile_fields = lax.dynamic_slice_in_dim(fields, start, CELL_DEV, 1)
        result = analyse_tile(tile_fields, counts_flat[tile_number], index_flat[tile_number], value_flat[tile_number], weight_flat[tile_number])
        return lax.dynamic_update_slice_in_dim(output, result.astype(output.dtype), start, 1)
    output = jnp.zeros((K, NCELL), jnp.bfloat16)
    return lax.fori_loop(0, tile_total, one_tile, output)
```

```python
import functools

import jax
import jax.numpy as jnp
from jax import lax
from jax.experimental import pallas as pl
from jax.experimental.pallas import tpu as pltpu
from jax.sharding import PartitionSpec as P

NS_ITERS = 6
MEAN_ROWS = 16
F32 = jnp.float32
BF16 = jnp.bfloat16


def dot(left, right, contract=((1,), (0,))):
    return lax.dot_general(left, right, (contract, ((), ())), preferred_element_type=F32)


def newton_steps(iterates, eye):
    roots = [None] * len(iterates)
    for step in range(NS_ITERS):
        products = iterates if step == 0 else [dot(r, y) for r, y in zip(roots, iterates)]
        factors = [(1.5 * eye - 0.5 * p.astype(F32)).astype(BF16) for p in products]
        if step < NS_ITERS - 1:
            iterates = [dot(y, f).astype(BF16) for y, f in zip(iterates, factors)]
        roots = factors if step == 0 else [dot(f, r).astype(BF16) for f, r in zip(factors, roots)]
    return roots


def analysis_kernel(count_ref, x_ref, index_ref, value_ref, weight_ref, out_ref, anomaly_s, mean_s, weight_s, pick_s):
    members, cells = x_ref.shape
    slots, nobs = index_ref.shape
    width = cells // slots
    x = x_ref[...].astype(F32)
    mean = jnp.sum(x, axis=0, keepdims=True) / members
    anomaly_s[:members, :] = (x - mean).astype(BF16)
    high = mean.astype(BF16).astype(F32)
    middle = (mean - high).astype(BF16).astype(F32)
    low = mean - high - middle
    row = lax.broadcasted_iota(jnp.int32, (MEAN_ROWS, cells), 0)
    parts = jnp.where(row == 0, high, jnp.where(row == 1, middle, jnp.where(row == 2, low, 0.0)))
    anomaly_s[members:, :] = parts.astype(BF16)
    for j in range(slots):
        mean_s[j : j + 1, :] = mean[:, j * width : (j + 1) * width]
    weight_s[...] = weight_ref[...].astype(F32)
    count = count_ref[0]
    square = (members, members)
    eye = (lax.broadcasted_iota(jnp.int32, square, 0) == lax.broadcasted_iota(jnp.int32, square, 1)).astype(F32)
    cell_ids = lax.broadcasted_iota(jnp.int32, (width, nobs), 0)
    lane = lax.broadcasted_iota(jnp.int32, (members, width), 1)
    iterates, scales, rights = [], [], []
    for block in range(slots):
        slot = (block * count) // slots
        index = index_ref[pl.ds(slot, 1), :]
        weight = weight_s[pl.ds(slot, 1), :]
        value = value_ref[pl.ds(slot, 1), :]
        within, part = lax.rem(index, width), lax.div(index, width)
        one_hot = (cell_ids == within).astype(F32).astype(BF16)
        for j in range(slots):
            pick_s[block, j * width : (j + 1) * width, :] = one_hot * (part == j).astype(F32).astype(BF16)
        picked = dot(anomaly_s[...], pick_s[block])
        observed = picked[:members]
        obs_mean = picked[members : members + 1] + picked[members + 1 : members + 2] + picked[members + 2 : members + 3]
        innovation = (weight * (value - obs_mean)).astype(BF16).astype(F32)
        weighted = (observed * weight).astype(BF16)
        rights.append(jnp.sum(observed * innovation, axis=1, keepdims=True))
        gram = dot(weighted, observed.astype(BF16), ((1,), (1,))) + (members - 1.0) * eye
        scale = jnp.sqrt(jnp.sum(jnp.sum(gram * gram, axis=0, keepdims=True), axis=1, keepdims=True))
        scales.append(scale)
        iterates.append((gram * (1.0 / scale)).astype(BF16))
    roots = newton_steps(iterates, eye)
    for block in range(slots):
        cols = slice(block * width, (block + 1) * width)
        root, right, scale = roots[block], rights[block], scales[block]
        high = right.astype(BF16).astype(F32)
        columns = jnp.where(lane == 0, high, jnp.where(lane == 1, right - high, 0.0)).astype(BF16)
        inner = dot(root, columns)
        inner = inner[:, 0:1] + inner[:, 1:2]
        moved = dot(root, anomaly_s[:members, cols], ((0,), (0,)))
        shift = jnp.sum(moved * inner, axis=0, keepdims=True) / scale + mean_s[block : block + 1, :]
        out_ref[:, cols] = (jnp.sqrt((members - 1.0) / scale) * moved + shift).astype(BF16)


def analyse(tile_fields, count, index, value, weight):
    members, cells = tile_fields.shape
    slots, nobs = index.shape
    vmem = pl.BlockSpec(memory_space=pltpu.VMEM)
    return pl.pallas_call(
        analysis_kernel,
        out_shape=jax.ShapeDtypeStruct((members, cells), BF16),
        in_specs=[pl.BlockSpec(memory_space=pltpu.SMEM)] + [vmem] * 4,
        out_specs=vmem,
        scratch_shapes=[
            pltpu.VMEM((members + MEAN_ROWS, cells), BF16),
            pltpu.VMEM((slots, cells // slots), F32),
            pltpu.VMEM((slots, nobs), F32),
            pltpu.VMEM((slots, cells, nobs), BF16),
        ],
        compiler_params=pltpu.CompilerParams(vmem_limit_bytes=48 << 20),
    )(count, tile_fields, index, value, weight)


def per_device(fields, counts, obs_index, obs_value, obs_weight):
    tile_fields = lax.all_to_all(fields, "wide", split_axis=1, concat_axis=0, tiled=True)
    count = lax.dynamic_slice(counts[:, 0], (lax.axis_index("narrow"),), (1,))
    result = analyse(tile_fields, count, obs_index[0, 0], obs_value[0, 0], obs_weight[0, 0])
    return lax.all_to_all(result, "wide", split_axis=0, concat_axis=1, tiled=True)


def solution(mesh):
    return jax.shard_map(
        per_device,
        mesh=mesh,
        in_specs=(
            P("wide", "narrow"),
            P(None, "wide"),
            P("narrow", "wide", None, None),
            P("narrow", "wide", None, None),
            P("narrow", "wide", None, None),
        ),
        out_specs=P("wide", "narrow"),
        check_vma=False,
    )
```

```python
import functools

import jax
import jax.numpy as jnp
from jax import lax
from jax.experimental import pallas as pl
from jax.experimental.pallas import tpu as pltpu
from jax.sharding import PartitionSpec as P


NS_ITERS = 6
PARTNERS = (6, 5, 3, 7, 2, 4, 1)
PACKED_ROWS = 16
F32 = jnp.float32
BF16 = jnp.bfloat16
VMEM = pl.BlockSpec(memory_space=pltpu.VMEM)
SMEM = pl.BlockSpec(memory_space=pltpu.SMEM)


def dot(left, right, contract=((1,), (0,))):
    return lax.dot_general(left, right, (contract, ((), ())), preferred_element_type=F32)


def pick_rows(rows, index, pick_s, slots):
    cells, nobs = pick_s.shape
    width = cells // slots
    cell_ids = lax.broadcasted_iota(jnp.int32, (width, nobs), 0)
    within, part = lax.rem(index, width), lax.div(index, width)
    one_hot = (cell_ids == within).astype(F32).astype(BF16)
    for j in range(slots):
        pick_s[j * width : (j + 1) * width, :] = one_hot * (part == j).astype(F32).astype(BF16)
    return dot(rows, pick_s[...])


def early_kernel(parts, count_ref, index_ref, value_ref, weight_ref, *refs):
    chunk_refs = refs[:parts]
    picked_ref, total_ref, index_out, value_out, weight_out, weight_s, pick_s = refs[parts:]
    slots, nobs = index_ref.shape
    count = count_ref[0]
    weight_s[...] = weight_ref[...].astype(F32)
    rows = jnp.concatenate([ref[...] for ref in chunk_refs], axis=0)
    for block in range(slots):
        slot = (block * count) // slots
        index = index_ref[pl.ds(slot, 1), :]
        index_out[block : block + 1, :] = index
        value_out[block : block + 1, :] = value_ref[pl.ds(slot, 1), :]
        weight_out[block : block + 1, :] = weight_s[pl.ds(slot, 1), :]
        picked = pick_rows(rows, index, pick_s.at[block % 2], slots)
        total_ref[block : block + 1, :] = jnp.sum(picked, axis=0, keepdims=True)
        picked_ref[:, block * nobs : (block + 1) * nobs] = picked.astype(BF16)


def newton_steps(iterates, eye):
    roots = [None] * len(iterates)
    for step in range(NS_ITERS):
        products = iterates if step == 0 else [dot(r, y) for r, y in zip(roots, iterates)]
        factors = [(1.5 * eye - 0.5 * p.astype(F32)).astype(BF16) for p in products]
        if step < NS_ITERS - 1:
            iterates = [dot(y, f).astype(BF16) for y, f in zip(iterates, factors)]
        roots = factors if step == 0 else [dot(f, r).astype(BF16) for f, r in zip(factors, roots)]
    return roots


def main_kernel(parts, early, index_ref, value_ref, weight_ref, picked_ref, total_ref, *refs):
    chunk_refs, out_refs = refs[:parts], refs[parts : 2 * parts]
    anomaly_s, mean_s, pick_s = refs[2 * parts :]
    share, cells = chunk_refs[0].shape
    members = share * parts
    slots, nobs = index_ref.shape
    width = cells // slots
    total = sum(jnp.sum(ref[...].astype(F32), axis=0, keepdims=True) for ref in chunk_refs)
    mean = total / members
    for p, ref in enumerate(chunk_refs):
        anomaly_s[p * share : (p + 1) * share, :] = (ref[...].astype(F32) - mean).astype(BF16)
    for j in range(slots):
        mean_s[j : j + 1, :] = mean[:, j * width : (j + 1) * width]
    square = (members, members)
    eye = (lax.broadcasted_iota(jnp.int32, square, 0) == lax.broadcasted_iota(jnp.int32, square, 1)).astype(F32)
    late = jnp.concatenate([ref[...] for ref in chunk_refs[early:]], axis=0)
    extra = lax.broadcasted_iota(jnp.int32, (PACKED_ROWS, nobs), 0) == 0
    iterates, scales, rights = [], [], []
    for block in range(slots):
        line = slice(block, block + 1)
        weight = weight_ref[line, :]
        picked = pick_rows(late, index_ref[line, :], pick_s.at[block % 2], slots)
        obs_mean = (total_ref[line, :] + jnp.sum(picked, axis=0, keepdims=True)) / members
        innovation = weight * (value_ref[line, :] - obs_mean)
        before = picked_ref[:, block * nobs : (block + 1) * nobs].astype(F32)
        observed = jnp.concatenate([(before - obs_mean).astype(BF16), (picked - obs_mean).astype(BF16)], axis=0)
        weighted = (observed.astype(F32) * weight).astype(BF16)
        left = jnp.concatenate([weighted, jnp.where(extra, innovation, 0.0).astype(BF16)], axis=0)
        products = dot(left, observed, ((1,), (1,)))
        rights.append(products[members : members + 1])
        gram = products[:members] + (members - 1.0) * eye
        scale = jnp.sqrt(jnp.sum(jnp.sum(gram * gram, axis=0, keepdims=True), axis=1, keepdims=True))
        scales.append(scale)
        iterates.append((gram * (1.0 / scale)).astype(BF16))
    roots = newton_steps(iterates, eye)
    for block in range(slots):
        cols = slice(block * width, (block + 1) * width)
        root, right, scale = roots[block], rights[block], scales[block]
        inner = jnp.sum(root.astype(F32) * right, axis=1, keepdims=True)
        moved = dot(root, anomaly_s[:, cols], ((0,), (0,)))
        shift = jnp.sum(moved * inner, axis=0, keepdims=True) / scale + mean_s[block : block + 1, :]
        result = (jnp.sqrt((members - 1.0) / scale) * moved + shift).astype(BF16)
        for p, ref in enumerate(out_refs):
            ref[:, cols] = result[p * share : (p + 1) * share]


def analyse(chunks, early, count, index, value, weight):
    parts = len(chunks)
    share, cells = chunks[0].shape
    slots, nobs = index.shape
    line = jax.ShapeDtypeStruct((slots, nobs), F32)
    rows = share * early
    picked, total, index, value, weight = pl.pallas_call(
        functools.partial(early_kernel, early),
        out_shape=[
            jax.ShapeDtypeStruct((rows, slots * nobs), BF16),
            line,
            jax.ShapeDtypeStruct((slots, nobs), jnp.int32),
            line,
            line,
        ],
        in_specs=[SMEM] + [VMEM] * (3 + early),
        out_specs=[VMEM] * 5,
        scratch_shapes=[pltpu.VMEM((slots, nobs), F32), pltpu.VMEM((2, cells, nobs), BF16)],
        cost_estimate=pl.CostEstimate(
            flops=2 * rows * cells * slots * nobs, bytes_accessed=rows * slots * nobs * 2, transcendentals=0
        ),
        compiler_params=pltpu.CompilerParams(vmem_limit_bytes=16 << 20),
    )(count, index, value, weight, *chunks[:early])
    return pl.pallas_call(
        functools.partial(main_kernel, parts, early),
        out_shape=[jax.ShapeDtypeStruct((share, cells), BF16)] * parts,
        in_specs=[VMEM] * (5 + parts),
        out_specs=[VMEM] * parts,
        scratch_shapes=[
            pltpu.VMEM((share * parts, cells), BF16),
            pltpu.VMEM((slots, cells // slots), F32),
            pltpu.VMEM((2, cells, nobs), BF16),
        ],
        compiler_params=pltpu.CompilerParams(vmem_limit_bytes=40 << 20),
    )(index, value, weight, picked, total, *chunks)


def partner_order(parts):
    return tuple(s for s in PARTNERS if s < parts) + tuple(range(len(PARTNERS) + 1, parts))


def by_permutes(parts, share):
    return parts & (parts - 1) == 0 and share % PACKED_ROWS == 0


def exchange(block, step):
    return lax.ppermute(block, "wide", [(i, i ^ step) for i in range(lax.axis_size("wide"))])


def per_device(fields, counts, obs_index, obs_value, obs_weight):
    parts, me = lax.axis_size("wide"), lax.axis_index("wide")
    share, width = fields.shape
    cells = width // parts
    count = lax.dynamic_slice(counts[:, 0], (lax.axis_index("narrow"),), (1,))
    tile = (count, obs_index[0, 0], obs_value[0, 0], obs_weight[0, 0])
    if not by_permutes(parts, share):
        whole = lax.all_to_all(fields, "wide", split_axis=1, concat_axis=0, tiled=True)
        half = whole.shape[0] // 2
        result = jnp.concatenate(analyse([whole[:half], whole[half:]], 1, *tile), axis=0)
        return lax.all_to_all(result, "wide", split_axis=0, concat_axis=1, tiled=True)
    order = partner_order(parts)
    steps = (0,) + order
    blocks = [lax.dynamic_slice(fields, (0, (me ^ s) * cells), (share, cells)) for s in steps]
    chunks = [blocks[0]] + [exchange(b, s) for b, s in zip(blocks[1:], order)]
    results = analyse(chunks, parts // 2, *tile)
    returned = [results[0]] + [exchange(b, s) for b, s in zip(results[1:], order)]
    analysis = jnp.zeros_like(fields)
    for s, block in zip(steps, returned):
        analysis = lax.dynamic_update_slice(analysis, block, (0, (me ^ s) * cells))
    return analysis


def solution(mesh):
    return jax.shard_map(
        per_device,
        mesh=mesh,
        in_specs=(
            P("wide", "narrow"),
            P(None, "wide"),
            P("narrow", "wide", None, None),
            P("narrow", "wide", None, None),
            P("narrow", "wide", None, None),
        ),
        out_specs=P("wide", "narrow"),
        check_vma=False,
    )
```

```python
import functools

import jax
import jax.numpy as jnp
from jax import lax
from jax.experimental import pallas as pl
from jax.experimental.pallas import tpu as pltpu
from jax.sharding import PartitionSpec as P


NS_ITERS = 6
PARTNERS = (6, 5, 3, 7, 2, 4, 1)
PACKED_ROWS = 16
F32 = jnp.float32
BF16 = jnp.bfloat16
VMEM = pl.BlockSpec(memory_space=pltpu.VMEM)
SMEM = pl.BlockSpec(memory_space=pltpu.SMEM)


def dot(left, right, contract=((1,), (0,))):
    return lax.dot_general(left, right, (contract, ((), ())), preferred_element_type=F32)


def pick_rows(rows, index, pick_s, slots):
    cells, nobs = pick_s.shape
    width = cells // slots
    cell_ids = lax.broadcasted_iota(jnp.int32, (width, nobs), 0)
    within, part = lax.rem(index, width), lax.div(index, width)
    one_hot = (cell_ids == within).astype(F32).astype(BF16)
    for j in range(slots):
        pick_s[j * width : (j + 1) * width, :] = one_hot * (part == j).astype(F32).astype(BF16)
    return dot(rows, pick_s[...])


def early_kernel(parts, count_ref, index_ref, value_ref, weight_ref, *refs):
    chunk_refs = refs[:parts]
    picked_ref, total_ref, index_out, value_out, weight_out, weight_s, pick_s = refs[parts:]
    slots, nobs = index_ref.shape
    count = count_ref[0]
    weight_s[...] = weight_ref[...].astype(F32)
    rows = jnp.concatenate([ref[...] for ref in chunk_refs], axis=0)
    for block in range(slots):
        slot = (block * count) // slots
        index = index_ref[pl.ds(slot, 1), :]
        index_out[block : block + 1, :] = index
        value_out[block : block + 1, :] = value_ref[pl.ds(slot, 1), :]
        weight_out[block : block + 1, :] = weight_s[pl.ds(slot, 1), :]
        picked = pick_rows(rows, index, pick_s.at[block % 2], slots)
        total_ref[block : block + 1, :] = jnp.sum(picked, axis=0, keepdims=True)
        picked_ref[:, block * nobs : (block + 1) * nobs] = picked.astype(BF16)


def newton_steps(iterates, eye):
    roots = [None] * len(iterates)
    for step in range(NS_ITERS):
        products = iterates if step == 0 else [dot(r, y) for r, y in zip(roots, iterates)]
        factors = [(1.5 * eye - 0.5 * p.astype(F32)).astype(BF16) for p in products]
        if step < NS_ITERS - 1:
            iterates = [dot(y, f).astype(BF16) for y, f in zip(iterates, factors)]
        roots = factors if step == 0 else [dot(f, r).astype(BF16) for f, r in zip(factors, roots)]
    return roots


def main_kernel(parts, early, index_ref, value_ref, weight_ref, picked_ref, total_ref, *refs):
    chunk_refs, out_refs = refs[:parts], refs[parts : 2 * parts]
    anomaly_s, mean_s, late_s, pick_s = refs[2 * parts :]
    share, cells = chunk_refs[0].shape
    members = share * parts
    slots, nobs = index_ref.shape
    width = cells // slots
    total = sum(jnp.sum(ref[...].astype(F32), axis=0, keepdims=True) for ref in chunk_refs)
    mean = total / members
    for p, ref in enumerate(chunk_refs):
        anomaly_s[p * share : (p + 1) * share, :] = (ref[...].astype(F32) - mean).astype(BF16)
    for j in range(slots):
        mean_s[j : j + 1, :] = mean[:, j * width : (j + 1) * width]
    square = (members, members)
    eye = (lax.broadcasted_iota(jnp.int32, square, 0) == lax.broadcasted_iota(jnp.int32, square, 1)).astype(F32)
    late = jnp.concatenate([ref[...] for ref in chunk_refs[early:]], axis=0)
    extra = lax.broadcasted_iota(jnp.int32, (PACKED_ROWS, nobs), 0) == 0
    blocks = range(slots)
    lines = [slice(block, block + 1) for block in blocks]
    obs_means = []
    for block in blocks:
        picked = pick_rows(late, index_ref[lines[block], :], pick_s.at[block % 2], slots)
        obs_means.append((total_ref[lines[block], :] + jnp.sum(picked, axis=0, keepdims=True)) / members)
        late_s[:, block * nobs : (block + 1) * nobs] = picked.astype(BF16)
    products = []
    for block in blocks:
        cols = slice(block * nobs, (block + 1) * nobs)
        obs_mean, weight = obs_means[block], weight_ref[lines[block], :]
        innovation = weight * (value_ref[lines[block], :] - obs_mean)
        observed = jnp.concatenate(
            [(ref[:, cols].astype(F32) - obs_mean).astype(BF16) for ref in (picked_ref, late_s)], axis=0
        )
        weighted = observed * weight.astype(BF16)
        left = jnp.concatenate([weighted, jnp.where(extra, innovation, 0.0).astype(BF16)], axis=0)
        products.append(dot(left, observed, ((1,), (1,))))
    rights = [p[members : members + 1] for p in products]
    iterates, scales = [], []
    for block in blocks:
        gram = products[block][:members] + (members - 1.0) * eye
        scale = jnp.sqrt(jnp.sum(jnp.sum(gram * gram, axis=0, keepdims=True), axis=1, keepdims=True))
        scales.append(scale)
        iterates.append((gram * (1.0 / scale)).astype(BF16))
    roots = newton_steps(iterates, eye)
    moved = [dot(roots[k], anomaly_s[:, k * width : (k + 1) * width], ((0,), (0,))) for k in blocks]
    inner = [jnp.sum(roots[k].astype(F32) * rights[k], axis=1, keepdims=True) for k in blocks]
    for block in blocks:
        cols, scale = slice(block * width, (block + 1) * width), scales[block]
        shift = jnp.sum(moved[block] * inner[block], axis=0, keepdims=True) / scale + mean_s[lines[block], :]
        result = (jnp.sqrt((members - 1.0) / scale) * moved[block] + shift).astype(BF16)
        for p, ref in enumerate(out_refs):
            ref[:, cols] = result[p * share : (p + 1) * share]


def analyse(chunks, early, count, index, value, weight):
    parts = len(chunks)
    share, cells = chunks[0].shape
    slots, nobs = index.shape
    line = jax.ShapeDtypeStruct((slots, nobs), F32)
    rows = share * early
    picked, total, index, value, weight = pl.pallas_call(
        functools.partial(early_kernel, early),
        out_shape=[
            jax.ShapeDtypeStruct((rows, slots * nobs), BF16),
            line,
            jax.ShapeDtypeStruct((slots, nobs), jnp.int32),
            line,
            line,
        ],
        in_specs=[SMEM] + [VMEM] * (3 + early),
        out_specs=[VMEM] * 5,
        scratch_shapes=[pltpu.VMEM((slots, nobs), F32), pltpu.VMEM((2, cells, nobs), BF16)],
        cost_estimate=pl.CostEstimate(
            flops=2 * rows * cells * slots * nobs, bytes_accessed=rows * slots * nobs * 2, transcendentals=0
        ),
        compiler_params=pltpu.CompilerParams(vmem_limit_bytes=16 << 20),
    )(count, index, value, weight, *chunks[:early])
    return pl.pallas_call(
        functools.partial(main_kernel, parts, early),
        out_shape=[jax.ShapeDtypeStruct((share, cells), BF16)] * parts,
        in_specs=[VMEM] * (5 + parts),
        out_specs=[VMEM] * parts,
        scratch_shapes=[
            pltpu.VMEM((share * parts, cells), BF16),
            pltpu.VMEM((slots, cells // slots), F32),
            pltpu.VMEM((share * (parts - early), slots * nobs), BF16),
            pltpu.VMEM((2, cells, nobs), BF16),
        ],
        compiler_params=pltpu.CompilerParams(vmem_limit_bytes=40 << 20),
    )(index, value, weight, picked, total, *chunks)


def partner_order(parts):
    return tuple(s for s in PARTNERS if s < parts) + tuple(range(len(PARTNERS) + 1, parts))


def by_permutes(parts, share):
    return parts & (parts - 1) == 0 and share % PACKED_ROWS == 0


def exchange(block, step):
    return lax.ppermute(block, "wide", [(i, i ^ step) for i in range(lax.axis_size("wide"))])


def per_device(fields, counts, obs_index, obs_value, obs_weight):
    parts, me = lax.axis_size("wide"), lax.axis_index("wide")
    share, width = fields.shape
    cells = width // parts
    count = lax.dynamic_slice(counts[:, 0], (lax.axis_index("narrow"),), (1,))
    tile = (count, obs_index[0, 0], obs_value[0, 0], obs_weight[0, 0])
    if not by_permutes(parts, share):
        whole = lax.all_to_all(fields, "wide", split_axis=1, concat_axis=0, tiled=True)
        half = whole.shape[0] // 2
        result = jnp.concatenate(analyse([whole[:half], whole[half:]], 1, *tile), axis=0)
        return lax.all_to_all(result, "wide", split_axis=0, concat_axis=1, tiled=True)
    order = partner_order(parts)
    steps = (0,) + order
    blocks = [lax.dynamic_slice(fields, (0, (me ^ s) * cells), (share, cells)) for s in steps]
    chunks = [blocks[0]] + [exchange(b, s) for b, s in zip(blocks[1:], order)]
    results = analyse(chunks, parts // 2, *tile)
    returned = [results[0]] + [exchange(b, s) for b, s in zip(results[1:], order)]
    analysis = jnp.zeros_like(fields)
    for s, block in zip(steps, returned):
        analysis = lax.dynamic_update_slice(analysis, block, (0, (me ^ s) * cells))
    return analysis


def solution(mesh):
    return jax.shard_map(
        per_device,
        mesh=mesh,
        in_specs=(
            P("wide", "narrow"),
            P(None, "wide"),
            P("narrow", "wide", None, None),
            P("narrow", "wide", None, None),
            P("narrow", "wide", None, None),
        ),
        out_specs=P("wide", "narrow"),
        check_vma=False,
    )
```

```python
import functools

import jax
import jax.numpy as jnp
from jax import lax
from jax.experimental import pallas as pl
from jax.experimental.pallas import tpu as pltpu
from jax.sharding import PartitionSpec as P


NS_ITERS = 6
PARTNERS = {"in": (6, 5, 3, 7, 2, 4, 1), "out": (7, 5, 6, 3, 2, 4, 1)}
PACKED_ROWS = 16
F32 = jnp.float32
BF16 = jnp.bfloat16
VMEM = pl.BlockSpec(memory_space=pltpu.VMEM)
SMEM = pl.BlockSpec(memory_space=pltpu.SMEM)


def dot(left, right, contract=((1,), (0,))):
    return lax.dot_general(left, right, (contract, ((), ())), preferred_element_type=F32)


def pick_rows(rows, index, pick_s, slots):
    cells, nobs = pick_s.shape
    width = cells // slots
    cell_ids = lax.broadcasted_iota(jnp.int32, (width, nobs), 0)
    within, part = lax.rem(index, width), lax.div(index, width)
    one_hot = (cell_ids == within).astype(F32).astype(BF16)
    for j in range(slots):
        pick_s[j * width : (j + 1) * width, :] = one_hot * (part == j).astype(F32).astype(BF16)
    return dot(rows, pick_s[...])


def early_kernel(parts, count_ref, index_ref, value_ref, weight_ref, *refs):
    chunk_refs = refs[:parts]
    picked_ref, index_out, value_out, weight_out, weight_s, pick_s = refs[parts:]
    slots, nobs = index_ref.shape
    count = count_ref[0]
    weight_s[...] = weight_ref[...].astype(F32)
    rows = jnp.concatenate([ref[...] for ref in chunk_refs], axis=0)
    for block in range(slots):
        slot = (block * count) // slots
        index = index_ref[pl.ds(slot, 1), :]
        index_out[block : block + 1, :] = index
        value_out[block : block + 1, :] = value_ref[pl.ds(slot, 1), :]
        weight_out[block : block + 1, :] = weight_s[pl.ds(slot, 1), :]
        picked = pick_rows(rows, index, pick_s.at[block % 2], slots)
        picked_ref[:, block * nobs : (block + 1) * nobs] = picked.astype(BF16)


def newton_steps(iterates, eye):
    roots = [None] * len(iterates)
    for step in range(NS_ITERS):
        if step == 0:
            factors = [(1.5 * eye).astype(BF16) - BF16(0.5) * y for y in iterates]
        else:
            factors = [(1.5 * eye - 0.5 * dot(r, y)).astype(BF16) for r, y in zip(roots, iterates)]
        if step < NS_ITERS - 1:
            iterates = [dot(y, f).astype(BF16) for y, f in zip(iterates, factors)]
        roots = factors if step == 0 else [dot(f, r).astype(BF16) for f, r in zip(factors, roots)]
    return roots


def main_kernel(parts, early, index_ref, value_ref, weight_ref, picked_ref, *refs):
    chunk_refs, out_refs = refs[:parts], refs[parts : 2 * parts]
    anomaly_s, mean_s, late_s, pick_s = refs[2 * parts :]
    share, cells = chunk_refs[0].shape
    members = share * parts
    slots, nobs = index_ref.shape
    width = cells // slots
    total = sum(jnp.sum(ref[...].astype(F32), axis=0, keepdims=True) for ref in chunk_refs)
    mean = total / members
    for p, ref in enumerate(chunk_refs):
        anomaly_s[p * share : (p + 1) * share, :] = (ref[...].astype(F32) - mean).astype(BF16)
    for j in range(slots):
        mean_s[j : j + 1, :] = mean[:, j * width : (j + 1) * width]
    square = (members, members)
    eye = (lax.broadcasted_iota(jnp.int32, square, 0) == lax.broadcasted_iota(jnp.int32, square, 1)).astype(F32)
    high = mean.astype(BF16).astype(F32)
    middle = (mean - high).astype(BF16).astype(F32)
    row = lax.broadcasted_iota(jnp.int32, (PACKED_ROWS, cells), 0)
    mean_rows = jnp.where(row == 0, high, jnp.where(row == 1, middle, jnp.where(row == 2, mean - high - middle, 0.0)))
    anomaly_s[members:, :] = mean_rows.astype(BF16)
    late = anomaly_s[share * early :, :]
    late_rows = members - share * early
    extra = lax.broadcasted_iota(jnp.int32, (PACKED_ROWS, nobs), 0) == 0
    blocks = range(slots)
    lines = [slice(block, block + 1) for block in blocks]
    obs_means = []
    for block in blocks:
        picked = pick_rows(late, index_ref[lines[block], :], pick_s.at[block % 2], slots)
        obs_means.append(sum(picked[late_rows + k : late_rows + k + 1] for k in range(3)))
        late_s[:, block * nobs : (block + 1) * nobs] = picked[:late_rows].astype(BF16)
    products = []
    for block in blocks:
        cols = slice(block * nobs, (block + 1) * nobs)
        obs_mean, weight = obs_means[block], weight_ref[lines[block], :]
        innovation = weight * (value_ref[lines[block], :] - obs_mean)
        before = (picked_ref[:, cols].astype(F32) - obs_mean).astype(BF16)
        observed = jnp.concatenate([before, late_s[:, cols]], axis=0)
        weighted = observed * weight.astype(BF16)
        left = jnp.concatenate([weighted, jnp.where(extra, innovation, 0.0).astype(BF16)], axis=0)
        products.append(dot(left, observed, ((1,), (1,))))
    rights = [p[members : members + 1] for p in products]
    iterates, scales = [], []
    for block in blocks:
        gram = products[block][:members] + (members - 1.0) * eye
        scale = jnp.sqrt(jnp.sum(jnp.sum(gram * gram, axis=0, keepdims=True), axis=1, keepdims=True))
        scales.append(scale)
        iterates.append((gram * (1.0 / scale)).astype(BF16))
    roots = newton_steps(iterates, eye)
    moved = [dot(roots[k], anomaly_s[:members, k * width : (k + 1) * width], ((0,), (0,))) for k in blocks]
    inner = [jnp.sum(roots[k].astype(F32) * rights[k], axis=1, keepdims=True) for k in blocks]
    for block in blocks:
        cols, scale = slice(block * width, (block + 1) * width), scales[block]
        shift = jnp.sum(moved[block] * inner[block], axis=0, keepdims=True) / scale + mean_s[lines[block], :]
        result = (jnp.sqrt((members - 1.0) / scale) * moved[block] + shift).astype(BF16)
        for p, ref in enumerate(out_refs):
            ref[:, cols] = result[p * share : (p + 1) * share]


def analyse(chunks, early, count, index, value, weight):
    parts = len(chunks)
    share, cells = chunks[0].shape
    slots, nobs = index.shape
    line = jax.ShapeDtypeStruct((slots, nobs), F32)
    rows = share * early
    picked, index, value, weight = pl.pallas_call(
        functools.partial(early_kernel, early),
        out_shape=[
            jax.ShapeDtypeStruct((rows, slots * nobs), BF16),
            jax.ShapeDtypeStruct((slots, nobs), jnp.int32),
            line,
            line,
        ],
        in_specs=[SMEM] + [VMEM] * (3 + early),
        out_specs=[VMEM] * 4,
        scratch_shapes=[pltpu.VMEM((slots, nobs), F32), pltpu.VMEM((2, cells, nobs), BF16)],
        cost_estimate=pl.CostEstimate(
            flops=2 * rows * cells * slots * nobs, bytes_accessed=rows * slots * nobs * 2, transcendentals=0
        ),
        compiler_params=pltpu.CompilerParams(vmem_limit_bytes=16 << 20),
    )(count, index, value, weight, *chunks[:early])
    return pl.pallas_call(
        functools.partial(main_kernel, parts, early),
        out_shape=[jax.ShapeDtypeStruct((share, cells), BF16)] * parts,
        in_specs=[VMEM] * (4 + parts),
        out_specs=[VMEM] * parts,
        scratch_shapes=[
            pltpu.VMEM((share * parts + PACKED_ROWS, cells), BF16),
            pltpu.VMEM((slots, cells // slots), F32),
            pltpu.VMEM((share * (parts - early), slots * nobs), BF16),
            pltpu.VMEM((2, cells, nobs), BF16),
        ],
        compiler_params=pltpu.CompilerParams(vmem_limit_bytes=40 << 20),
    )(index, value, weight, picked, *chunks)


def partner_order(way, parts):
    known = PARTNERS[way]
    return tuple(s for s in known if s < parts) + tuple(range(len(known) + 1, parts))


def by_permutes(parts, share):
    return parts & (parts - 1) == 0 and share % PACKED_ROWS == 0


def exchange(block, step):
    return lax.ppermute(block, "wide", [(i, i ^ step) for i in range(lax.axis_size("wide"))])


def per_device(fields, counts, obs_index, obs_value, obs_weight):
    parts, me = lax.axis_size("wide"), lax.axis_index("wide")
    share, width = fields.shape
    cells = width // parts
    count = lax.dynamic_slice(counts[:, 0], (lax.axis_index("narrow"),), (1,))
    tile = (count, obs_index[0, 0], obs_value[0, 0], obs_weight[0, 0])
    if not by_permutes(parts, share):
        whole = lax.all_to_all(fields, "wide", split_axis=1, concat_axis=0, tiled=True)
        half = whole.shape[0] // 2
        result = jnp.concatenate(analyse([whole[:half], whole[half:]], 1, *tile), axis=0)
        return lax.all_to_all(result, "wide", split_axis=0, concat_axis=1, tiled=True)
    order = partner_order("in", parts)
    steps = (0,) + order
    blocks = [lax.dynamic_slice(fields, (0, (me ^ s) * cells), (share, cells)) for s in steps]
    chunks = [blocks[0]] + [exchange(b, s) for b, s in zip(blocks[1:], order)]
    results = dict(zip(steps, analyse(chunks, parts // 2, *tile)))
    order = partner_order("out", parts)
    returned = [results[0]] + [exchange(results[s], s) for s in order]
    analysis = jnp.zeros_like(fields)
    for s, block in zip((0,) + order, returned):
        analysis = lax.dynamic_update_slice(analysis, block, (0, (me ^ s) * cells))
    return analysis


def solution(mesh):
    return jax.shard_map(
        per_device,
        mesh=mesh,
        in_specs=(
            P("wide", "narrow"),
            P(None, "wide"),
            P("narrow", "wide", None, None),
            P("narrow", "wide", None, None),
            P("narrow", "wide", None, None),
        ),
        out_specs=P("wide", "narrow"),
        check_vma=False,
    )
```

```python
import functools

import jax
import jax.numpy as jnp
from jax import lax
from jax.experimental import pallas as pl
from jax.experimental.pallas import tpu as pltpu
from jax.sharding import PartitionSpec as P


NS_ITERS = 6
PARTNERS = {"in": (6, 5, 3, 7, 2, 4, 1), "out": (7, 5, 6, 3, 2, 4, 1)}
PACKED_ROWS = 16
F32 = jnp.float32
BF16 = jnp.bfloat16
VMEM = pl.BlockSpec(memory_space=pltpu.VMEM)
SMEM = pl.BlockSpec(memory_space=pltpu.SMEM)


def dot(left, right, contract=((1,), (0,))):
    return lax.dot_general(left, right, (contract, ((), ())), preferred_element_type=F32)


def pick_rows(rows, index, pick_s, slots):
    cells, nobs = pick_s.shape
    width = cells // slots
    cell_ids = lax.broadcasted_iota(jnp.int32, (width, nobs), 0)
    within, part = lax.rem(index, width), lax.div(index, width)
    one_hot = (cell_ids == within).astype(F32).astype(BF16)
    for j in range(slots):
        pick_s[j * width : (j + 1) * width, :] = one_hot * (part == j).astype(F32).astype(BF16)
    return dot(rows, pick_s[...])


def early_kernel(parts, count_ref, index_ref, value_ref, weight_ref, *refs):
    chunk_refs = refs[:parts]
    picked_ref, index_out, value_out, weight_out, weight_s, pick_s = refs[parts:]
    slots, nobs = index_ref.shape
    count = count_ref[0]
    weight_s[...] = weight_ref[...].astype(F32)
    rows = jnp.concatenate([ref[...] for ref in chunk_refs], axis=0)
    for block in range(slots):
        slot = (block * count) // slots
        index = index_ref[pl.ds(slot, 1), :]
        index_out[block : block + 1, :] = index
        value_out[block : block + 1, :] = value_ref[pl.ds(slot, 1), :]
        weight_out[block : block + 1, :] = weight_s[pl.ds(slot, 1), :]
        picked = pick_rows(rows, index, pick_s.at[block % 2], slots)
        picked_ref[:, block * nobs : (block + 1) * nobs] = picked.astype(BF16)


def add_diagonal(matrix, eye, value):
    size, tile = matrix.shape[0], eye.shape[0]
    rows = []
    for i in range(0, size, tile):
        cells = [matrix[i : i + tile, j : j + tile] for j in range(0, size, tile)]
        rows.append(jnp.concatenate([c + value * eye if k * tile == i else c for k, c in enumerate(cells)], axis=1))
    return jnp.concatenate(rows, axis=0)


def newton_steps(iterates, eye):
    roots = [None] * len(iterates)
    for step in range(NS_ITERS):
        if step == 0:
            factors = [add_diagonal(BF16(-0.5) * y, eye.astype(BF16), BF16(1.5)) for y in iterates]
        else:
            factors = [add_diagonal(-0.5 * dot(r, y), eye, 1.5).astype(BF16) for r, y in zip(roots, iterates)]
        if step < NS_ITERS - 1:
            iterates = [dot(y, f).astype(BF16) for y, f in zip(iterates, factors)]
        roots = factors if step == 0 else [dot(f, r).astype(BF16) for f, r in zip(factors, roots)]
    return roots


def main_kernel(parts, early, index_ref, value_ref, weight_ref, picked_ref, *refs):
    chunk_refs, out_refs = refs[:parts], refs[parts : 2 * parts]
    anomaly_s, mean_s, late_s, pick_s = refs[2 * parts :]
    share, cells = chunk_refs[0].shape
    members = share * parts
    slots, nobs = index_ref.shape
    width = cells // slots
    total = sum(jnp.sum(ref[...].astype(F32), axis=0, keepdims=True) for ref in chunk_refs)
    mean = total / members
    for p, ref in enumerate(chunk_refs):
        anomaly_s[p * share : (p + 1) * share, :] = (ref[...].astype(F32) - mean).astype(BF16)
    for j in range(slots):
        mean_s[j : j + 1, :] = mean[:, j * width : (j + 1) * width]
    tile = 128 if members % 128 == 0 else members
    square = (tile, tile)
    eye = (lax.broadcasted_iota(jnp.int32, square, 0) == lax.broadcasted_iota(jnp.int32, square, 1)).astype(F32)
    high = mean.astype(BF16).astype(F32)
    middle = (mean - high).astype(BF16).astype(F32)
    row = lax.broadcasted_iota(jnp.int32, (PACKED_ROWS, cells), 0)
    mean_rows = jnp.where(row == 0, high, jnp.where(row == 1, middle, jnp.where(row == 2, mean - high - middle, 0.0)))
    anomaly_s[members:, :] = mean_rows.astype(BF16)
    late = anomaly_s[share * early :, :]
    late_rows = members - share * early
    extra = lax.broadcasted_iota(jnp.int32, (PACKED_ROWS, nobs), 0) == 0
    blocks = range(slots)
    lines = [slice(block, block + 1) for block in blocks]
    obs_means = []
    for block in blocks:
        picked = pick_rows(late, index_ref[lines[block], :], pick_s.at[block % 2], slots)
        obs_means.append(sum(picked[late_rows + k : late_rows + k + 1] for k in range(3)))
        late_s[:, block * nobs : (block + 1) * nobs] = picked[:late_rows].astype(BF16)
    products = []
    for block in blocks:
        cols = slice(block * nobs, (block + 1) * nobs)
        obs_mean, weight = obs_means[block], weight_ref[lines[block], :]
        innovation = weight * (value_ref[lines[block], :] - obs_mean)
        before = (picked_ref[:, cols].astype(F32) - obs_mean).astype(BF16)
        observed = jnp.concatenate([before, late_s[:, cols]], axis=0)
        weighted = observed * weight.astype(BF16)
        left = jnp.concatenate([weighted, jnp.where(extra, innovation, 0.0).astype(BF16)], axis=0)
        products.append(dot(left, observed, ((1,), (1,))))
    rights = [p[members : members + 1] for p in products]
    iterates, scales = [], []
    for block in blocks:
        gram = add_diagonal(products[block][:members], eye, members - 1.0)
        scale = jnp.sqrt(jnp.sum(jnp.sum(gram * gram, axis=0, keepdims=True), axis=1, keepdims=True))
        scales.append(scale)
        iterates.append((gram * (1.0 / scale)).astype(BF16))
    roots = newton_steps(iterates, eye)
    moved = [dot(roots[k], anomaly_s[:members, k * width : (k + 1) * width], ((0,), (0,))) for k in blocks]
    inner = [jnp.sum(roots[k].astype(F32) * rights[k], axis=1, keepdims=True) for k in blocks]
    for block in blocks:
        cols, scale = slice(block * width, (block + 1) * width), scales[block]
        shift = jnp.sum(moved[block] * inner[block], axis=0, keepdims=True) / scale + mean_s[lines[block], :]
        result = (jnp.sqrt((members - 1.0) / scale) * moved[block] + shift).astype(BF16)
        for p, ref in enumerate(out_refs):
            ref[:, cols] = result[p * share : (p + 1) * share]


def analyse(chunks, early, count, index, value, weight):
    parts = len(chunks)
    share, cells = chunks[0].shape
    slots, nobs = index.shape
    line = jax.ShapeDtypeStruct((slots, nobs), F32)
    rows = share * early
    picked, index, value, weight = pl.pallas_call(
        functools.partial(early_kernel, early),
        out_shape=[
            jax.ShapeDtypeStruct((rows, slots * nobs), BF16),
            jax.ShapeDtypeStruct((slots, nobs), jnp.int32),
            line,
            line,
        ],
        in_specs=[SMEM] + [VMEM] * (3 + early),
        out_specs=[VMEM] * 4,
        scratch_shapes=[pltpu.VMEM((slots, nobs), F32), pltpu.VMEM((2, cells, nobs), BF16)],
        cost_estimate=pl.CostEstimate(
            flops=2 * rows * cells * slots * nobs, bytes_accessed=rows * slots * nobs * 2, transcendentals=0
        ),
        compiler_params=pltpu.CompilerParams(vmem_limit_bytes=16 << 20),
    )(count, index, value, weight, *chunks[:early])
    return pl.pallas_call(
        functools.partial(main_kernel, parts, early),
        out_shape=[jax.ShapeDtypeStruct((share, cells), BF16)] * parts,
        in_specs=[VMEM] * (4 + parts),
        out_specs=[VMEM] * parts,
        scratch_shapes=[
            pltpu.VMEM((share * parts + PACKED_ROWS, cells), BF16),
            pltpu.VMEM((slots, cells // slots), F32),
            pltpu.VMEM((share * (parts - early), slots * nobs), BF16),
            pltpu.VMEM((2, cells, nobs), BF16),
        ],
        compiler_params=pltpu.CompilerParams(vmem_limit_bytes=40 << 20),
    )(index, value, weight, picked, *chunks)


def partner_order(way, parts):
    known = PARTNERS[way]
    return tuple(s for s in known if s < parts) + tuple(range(len(known) + 1, parts))


def by_permutes(parts, share):
    return parts & (parts - 1) == 0 and share % PACKED_ROWS == 0


def exchange(block, step):
    return lax.ppermute(block, "wide", [(i, i ^ step) for i in range(lax.axis_size("wide"))])


def per_device(fields, counts, obs_index, obs_value, obs_weight):
    parts, me = lax.axis_size("wide"), lax.axis_index("wide")
    share, width = fields.shape
    cells = width // parts
    count = lax.dynamic_slice(counts[:, 0], (lax.axis_index("narrow"),), (1,))
    tile = (count, obs_index[0, 0], obs_value[0, 0], obs_weight[0, 0])
    if not by_permutes(parts, share):
        whole = lax.all_to_all(fields, "wide", split_axis=1, concat_axis=0, tiled=True)
        half = whole.shape[0] // 2
        result = jnp.concatenate(analyse([whole[:half], whole[half:]], 1, *tile), axis=0)
        return lax.all_to_all(result, "wide", split_axis=0, concat_axis=1, tiled=True)
    order = partner_order("in", parts)
    steps = (0,) + order
    blocks = [lax.dynamic_slice(fields, (0, (me ^ s) * cells), (share, cells)) for s in steps]
    chunks = [blocks[0]] + [exchange(b, s) for b, s in zip(blocks[1:], order)]
    results = dict(zip(steps, analyse(chunks, parts // 2, *tile)))
    order = partner_order("out", parts)
    returned = [results[0]] + [exchange(results[s], s) for s in order]
    analysis = jnp.zeros_like(fields)
    for s, block in zip((0,) + order, returned):
        analysis = lax.dynamic_update_slice(analysis, block, (0, (me ^ s) * cells))
    return analysis


def solution(mesh):
    return jax.shard_map(
        per_device,
        mesh=mesh,
        in_specs=(
            P("wide", "narrow"),
            P(None, "wide"),
            P("narrow", "wide", None, None),
            P("narrow", "wide", None, None),
            P("narrow", "wide", None, None),
        ),
        out_specs=P("wide", "narrow"),
        check_vma=False,
    )
```
